32 devices in a mesh: tensor: 4 (over x, core), context: 8 (over z, y).
Axes of the slice: x: 2, y: 2, z: 4, core: 2. Of those that a mesh axis runs over, the one named last changes fastest.
Arguments:
- query_states: bfloat16 [2048, 512], P('context', 'tensor'), may hold values from -6 to 6
- key_states: bfloat16 [2048, 512], P('context', 'tensor'), may hold values from -6 to 6
- value_states: bfloat16 [2048, 512], P('context', 'tensor'), may hold values from -6 to 6
- out_grad: bfloat16 [2048, 6144], P('context', 'tensor'), may hold values from -6 to 6
- out_proj: bfloat16 [6144, 512], P(None, 'tensor'), may hold values from -0.25 to 0.25
Outputs:
- query_grad: bfloat16 [2048, 512], P('context', 'tensor')
- key_grad: bfloat16 [2048, 512], P('context', 'tensor')
- value_grad: bfloat16 [2048, 512], P('context', 'tensor')
- proj_grad: float32 [6144, 512], P('context', 'tensor')
The draws below stay inside these ranges and needn't reach their ends.
All inputs are finite; a program needn't handle non-finite values.
Results may differ from the reference program's by a relative error of at most 0.038.
Values may be sent and summed in bfloat16 or wider, within the bound.
No kernel may reach another device: no remote copies, remote signals or barrier semaphores. Data moves between devices by JAX's collectives and lax.ppermute only.
A program may use at most 128 MiB of HBM per device.

```python
import math
import jax
import jax.numpy as jnp
from jax import lax

D = 6144
HD = 128
HEADS = 4
TOKENS = 2048


def draw_query_states(key, part):
    columns = HEADS * HD
    values = jnp.clip(1.2 * jax.random.normal(jax.random.fold_in(key, 11), (TOKENS, columns), jnp.float32), -6.0, 6.0)
    return values.astype(jnp.bfloat16)


def draw_key_states(key, part):
    columns = HEADS * HD
    values = jnp.clip(1.2 * jax.random.normal(jax.random.fold_in(key, 12), (TOKENS, columns), jnp.float32), -6.0, 6.0)
    return values.astype(jnp.bfloat16)


def strengthened(array, key, source, target, parts, factor):
    owner, partner = [(jnp.arange(array.shape[position]) // (array.shape[position] // parts)).reshape([-1 if axis == position else 1 for axis in range(array.ndim)]) for position in (source, target)]
    chosen = jax.random.permutation(key, parts)[partner]
    strong = (owner == chosen) | (owner == (partner + parts // 2) % parts)
    return jnp.where(strong, factor * array, array)


def block_scale(stream_key, shape, pieces, smallest, largest):
    level = 1.0
    for dim, blocks in pieces:
        heights = jax.random.uniform(jax.random.fold_in(jax.random.fold_in(stream_key, 6), dim), (blocks,), jnp.float32, smallest / len(pieces), largest / len(pieces))
        level = level * jnp.repeat(jnp.exp(heights), shape[dim] // blocks).reshape((-1,) + (1,) * (len(shape) - 1 - dim))
    return level


def bell_draw(own_key, extent, scale, reach, pieces=(), dtype=jnp.bfloat16):
    values = scale * jax.random.normal(own_key, extent, jnp.float32)
    if pieces:
        values = values * block_scale(own_key, extent, pieces, -0.22, 0.18)
    return jnp.clip(values, -reach, reach).astype(dtype)


def gaussian_with(own_key, shape, scale, most, shards, heavy, dtype=jnp.bfloat16):
    drawn = scale * jax.random.normal(own_key, shape, jnp.float32)
    if shards:
        drawn = drawn * block_scale(own_key, shape, shards, -0.22, 0.18)
    return jnp.clip(strengthened(drawn, jax.random.fold_in(own_key, 3), *heavy), -most, most).astype(dtype)


def setup_inputs(seed: int = 0) -> dict:
    arg_keys = jax.random.split(jax.random.key(seed), 6)
    return {
        "query_states": draw_query_states(jax.random.fold_in(arg_keys[5], 71), 0),
        "key_states": draw_key_states(jax.random.fold_in(arg_keys[5], 71), 0),
        "value_states": bell_draw(arg_keys[2], (TOKENS, HEADS * HD), 1.0, 6.0, ((0, 8), (1, 4))),
        "out_grad": gaussian_with(arg_keys[3], (TOKENS, D), 1.0, 6.0, ((0, 8), (1, 4)), (0, 1, 8, 2.0)),
        "out_proj": bell_draw(arg_keys[4], (D, HEADS * HD), (HEADS * HD) ** -0.5, 0.25, ((1, 4),)),
    }


log_two_e = 1.4426950408889634


def reference(query_states, key_states, value_states, out_grad, out_proj):
    scaling = HD ** -0.5
    score_scale = scaling * log_two_e
    block_rows = math.gcd(TOKENS, 1024)
    block_count = TOKENS // block_rows
    attended_grad = jnp.dot(out_grad, out_proj, preferred_element_type=jnp.float32).astype(jnp.bfloat16)
    attended_parts = []
    query_parts = []
    key_parts = []
    value_parts = []
    for head_index in range(HEADS):
        first_column = head_index * HD
        query_head = query_states[:, first_column:first_column + HD]
        key_head = key_states[:, first_column:first_column + HD]
        value_head = value_states[:, first_column:first_column + HD]
        grad_head = attended_grad[:, first_column:first_column + HD]

        def forward_rows(query_block, key_head=key_head, value_head=value_head):
            scores = jnp.dot(query_block, key_head.T, preferred_element_type=jnp.float32) * score_scale
            row_shift = jnp.ceil(jnp.max(scores, axis=1))
            powers = jnp.exp2(scores - row_shift[:, None])
            row_total = jnp.sum(powers, axis=1)
            weighted = jnp.dot(powers.astype(jnp.bfloat16), value_head, preferred_element_type=jnp.float32)
            return (weighted / row_total[:, None]).astype(jnp.bfloat16), row_shift + jnp.log2(row_total)

        attended_head, log_total = lax.map(forward_rows, query_head.reshape(block_count, block_rows, HD))
        attended_head = attended_head.reshape(TOKENS, HD)
        log_total = log_total.reshape(TOKENS)
        row_delta = jnp.sum(attended_head.astype(jnp.float32) * grad_head.astype(jnp.float32), axis=1)

        def backward_rows(running, inputs, key_head=key_head, value_head=value_head):
            query_block, grad_block, total_block, delta_block = inputs
            scores = jnp.dot(query_block, key_head.T, preferred_element_type=jnp.float32) * score_scale
            weights = jnp.exp2(scores - total_block[:, None])
            prob_grad = jnp.dot(grad_block, value_head.T, preferred_element_type=jnp.float32)
            score_grad = (weights * (prob_grad - delta_block[:, None])).astype(jnp.bfloat16)
            block_grad = (jnp.dot(score_grad, key_head, preferred_element_type=jnp.float32) * scaling).astype(jnp.bfloat16)
            key_sum = running[0] + jnp.dot(score_grad.T, query_block, preferred_element_type=jnp.float32)
            value_sum = running[1] + jnp.dot(weights.astype(jnp.bfloat16).T, grad_block, preferred_element_type=jnp.float32)
            return (key_sum, value_sum), block_grad

        empty_sum = jnp.zeros((TOKENS, HD), jnp.float32)
        sequences = (query_head.reshape(block_count, block_rows, HD), grad_head.reshape(block_count, block_rows, HD),
                     log_total.reshape(block_count, block_rows), row_delta.reshape(block_count, block_rows))
        (key_sum, value_sum), query_head_grad = lax.scan(backward_rows, (empty_sum, empty_sum), sequences)
        attended_parts.append(attended_head)
        query_parts.append(query_head_grad.reshape(TOKENS, HD))
        key_parts.append((key_sum * scaling).astype(jnp.bfloat16))
        value_parts.append(value_sum.astype(jnp.bfloat16))
    attended = jnp.concatenate(attended_parts, axis=1)
    proj_grad = jnp.dot(out_grad.T, attended, preferred_element_type=jnp.float32)
    return (jnp.concatenate(query_parts, axis=1), jnp.concatenate(key_parts, axis=1),
            jnp.concatenate(value_parts, axis=1), proj_grad)
```

```python
import functools

import jax
import jax.numpy as jnp
from jax import lax
from jax.experimental import pallas as pl
from jax.experimental.pallas import tpu as pltpu
from jax.sharding import PartitionSpec as P

HD = 128
SCALING = HD ** (-0.5)
LOG_TWO_E = 1.4426950408889634
SCORE_SCALE = SCALING * LOG_TWO_E
F32 = jnp.float32
BF16 = jnp.bfloat16


def mm(a, b, dims):
    return lax.dot_general(a, b, (dims, ((), ())), preferred_element_type=F32)


NN = ((1,), (0,))
NT = ((1,), (1,))
TN = ((0,), (0,))


def call(kernel, outs, scratch, flops, nbytes):
    vmem = pl.BlockSpec(memory_space=pltpu.VMEM)

    def run(*args):
        return pl.pallas_call(
            kernel,
            out_shape=[jax.ShapeDtypeStruct(s, d) for s, d in outs],
            in_specs=[vmem] * len(args),
            out_specs=[vmem] * len(outs),
            scratch_shapes=scratch,
            cost_estimate=pl.CostEstimate(flops=flops, bytes_accessed=nbytes, transcendentals=0),
        )(*args)

    return run


def forward_kernel(groups, *refs):
    q_own, q_peer = refs[0], refs[1]
    kv = refs[2 : 2 + groups]
    packed, scores = refs[2 + groups], refs[3 + groups]
    rows = q_own.shape[0]
    q = jnp.concatenate([q_own[...], q_peer[...]], axis=0)
    top = None
    for j in range(groups):
        block = mm(kv[j][:, :HD], q, NT) * SCORE_SCALE
        scores[j] = block
        peak = jnp.max(block, axis=0, keepdims=True)
        top = peak if top is None else jnp.maximum(top, peak)
    shift = jnp.ceil(top)
    total = jnp.zeros((1, 2 * rows), F32)
    out = jnp.zeros((HD, 2 * rows), F32)
    for j in range(groups):
        powers = jnp.exp2(scores[j] - shift)
        total = total + jnp.sum(powers, axis=0, keepdims=True)
        out = out + mm(kv[j][:, HD:], powers.astype(BF16), TN)
    packed[:HD, :] = (out / total).astype(BF16)
    log_total = shift + jnp.log2(total)
    high = log_total.astype(BF16)
    rest = log_total - high.astype(F32)
    middle = rest.astype(BF16)
    low = (rest - middle.astype(F32)).astype(BF16)
    index = lax.broadcasted_iota(jnp.int32, (16, 2 * rows), 0)
    tail = jnp.where(index == 0, high.astype(F32), jnp.where(index == 1, middle.astype(F32), low.astype(F32)))
    packed[HD:, :] = tail.astype(BF16)


def log_total_of(packed):
    tail = packed[HD:, :].astype(F32)
    return tail[0:1, :] + tail[1:2, :] + tail[2:3, :]


def sources(tensor_size):
    return [(j, s) for s in range(2) for j in range(tensor_size // 2)]


def source_index(tensor_size, j, s):
    t = lax.axis_index("tensor")
    if s:
        t = t + 1 - 2 * lax.rem(t, 2)
    return lax.rem(t - 2 * j + tensor_size, tensor_size)


def grad_kernel(tensor_size, *refs):
    own = refs[:tensor_size]
    peer = refs[tensor_size : 2 * tensor_size]
    weight, out, sent = refs[2 * tensor_size :]
    rows = own[0].shape[0]
    sums = [jnp.zeros((rows, HD), F32), jnp.zeros((rows, HD), F32)]
    for i, (j, s) in enumerate(sources(tensor_size)):
        w = weight[source_index(tensor_size, j, s)]
        sums[0] = sums[0] + mm(own[i][...], w, NN)
        sums[1] = sums[1] + mm(peer[i][...], w, NN)
    for half in range(2):
        out[half * rows : (half + 1) * rows, :] = sums[half]
        sent[(1 - half) * rows : (2 - half) * rows, :] = sums[half].astype(BF16)


def proj_kernel(tensor_size, groups, span, *refs):
    own = refs[:tensor_size]
    peer = refs[tensor_size : 2 * tensor_size]
    mine, theirs = refs[2 * tensor_size : 2 * tensor_size + 2]
    rest = refs[2 * tensor_size + 2 :]
    attended_ref, log_ref = rest[:2]
    pieces = rest[2 : 2 + groups]
    parts = rest[2 + groups]
    rows = own[0].shape[0]
    log_mine = log_total_of(mine)
    log_theirs = log_total_of(theirs)
    log_theirs = jnp.concatenate([log_theirs[:, rows:], log_theirs[:, :rows]], axis=1)
    top = jnp.maximum(log_mine, log_theirs)
    low = jnp.minimum(log_mine, log_theirs)
    log_total = top + jnp.log2(1.0 + jnp.exp2(low - top))
    out_theirs = theirs[:HD, :].astype(F32)
    out_theirs = jnp.concatenate([out_theirs[:, rows:], out_theirs[:, :rows]], axis=1)
    attended = mine[:HD, :].astype(F32) * jnp.exp2(log_mine - log_total)
    attended = (attended + out_theirs * jnp.exp2(log_theirs - log_total)).astype(BF16)
    attended_ref[...] = attended
    log_ref[...] = jnp.broadcast_to(log_total, log_ref.shape)
    per_piece = groups // tensor_size
    for i, (j, s) in enumerate(sources(tensor_size)):
        part = mm(attended[:, :rows], own[i][...], NN) + mm(attended[:, rows:], peer[i][...], NN)
        first = source_index(tensor_size, j, s) * per_piece
        for n in range(per_piece):
            parts[first + n] = part[:, n * span : (n + 1) * span]
    outer = lax.div(lax.axis_index("context"), 2)
    pieces[0][...] = parts[outer]
    for n in range(1, groups):
        pieces[n][...] = parts[lax.rem(outer + n, groups)].astype(BF16)


def backward_kernel(groups, *refs):
    q_own, q_peer = refs[0], refs[1]
    kv = refs[2 : 2 + groups]
    grad_mine, grad_theirs, attended, log_ref = refs[2 + groups : 6 + groups]
    q_mine, q_theirs = refs[6 + groups : 8 + groups]
    pieces = refs[8 + groups : 8 + 2 * groups]
    rows = q_own.shape[0]
    q = jnp.concatenate([q_own[...], q_peer[...]], axis=0)
    grad = (grad_mine[...] + grad_theirs[...].astype(F32)).astype(BF16)
    log_total = log_ref[0:1, :]
    delta = jnp.sum(attended[...].astype(F32) * grad.astype(F32).T, axis=0, keepdims=True)
    q_sum = jnp.zeros((HD, 2 * rows), F32)
    for j in range(groups):
        key = kv[j][:, :HD]
        value = kv[j][:, HD:]
        weights = jnp.exp2(mm(key, q, NT) * SCORE_SCALE - log_total)
        score_grad = (weights * (mm(value, grad, NT) - delta)).astype(BF16)
        k_part = mm(score_grad, q, NN) * SCALING
        v_part = mm(weights.astype(BF16), grad, NN)
        pieces[j][:, :HD] = k_part.astype(pieces[j].dtype)
        pieces[j][:, HD:] = v_part.astype(pieces[j].dtype)
        q_sum = q_sum + mm(key, score_grad, TN)
    q_sum = q_sum * SCALING
    q_mine[...] = q_sum[:, :rows]
    q_theirs[...] = q_sum[:, rows:].astype(BF16)


def join_kernel(groups, *refs):
    q_mine, q_theirs = refs[0], refs[1]
    pieces = refs[2 : 2 + groups]
    q_out, k_out, v_out = refs[2 + groups :]
    q_out[...] = (q_mine[...] + q_theirs[...].astype(F32)).T.astype(BF16)
    total = pieces[0][...]
    for n in range(1, groups):
        total = total + pieces[n][...].astype(F32)
    k_out[...] = total[:, :HD].astype(BF16)
    v_out[...] = total[:, HD:].astype(BF16)


def proj_join_kernel(groups, *refs):
    total = refs[0][...]
    for n in range(1, groups):
        total = total + refs[n][...].astype(F32)
    refs[groups][...] = total.T


def local(tensor_size, context_size, query_states, key_states, value_states, out_grad, out_proj):
    groups = context_size // 2
    rows, width = out_grad.shape
    span = width * tensor_size // context_size
    inner = lax.rem(lax.axis_index("context"), 2)
    contexts = range(context_size)
    pair = [(c, c + 1 - 2 * (c % 2)) for c in contexts]
    sibling = [(t, t + 1 - 2 * (t % 2)) for t in range(tensor_size)]

    def shifted(array, n):
        return lax.ppermute(array, "context", [(c, (c + 2 * n) % context_size) for c in contexts])

    def columns(array, which, axis):
        if array.shape[axis] == 2 * span:
            return lax.dynamic_slice_in_dim(array, which * span, span, axis)
        split = array.reshape(array.shape[:axis] + (-1, 2, span) + array.shape[axis + 1 :])
        kept = lax.dynamic_index_in_dim(split, which, axis + 1, keepdims=False)
        return kept.reshape(array.shape[:axis] + (-1,) + array.shape[axis + 1 :])

    kv = jnp.concatenate([key_states, value_states], axis=1)
    kvs = [kv] + [shifted(kv, n) for n in range(1, groups)]
    q_peer = lax.ppermute(query_states, "context", pair)

    kept = columns(out_grad, inner, 1)
    given = columns(out_grad, 1 - inner, 1)
    own, peer = [], []
    for j in range(tensor_size // 2):
        to = [(t, (t + 2 * j) % tensor_size) for t in range(tensor_size)]
        both = [(t * context_size + c, u * context_size + d) for t, u in to for c, d in pair]
        own.append(lax.ppermute(kept, "tensor", to) if j else kept)
        peer.append(lax.ppermute(given, ("tensor", "context"), both))
    own = own + [lax.ppermute(piece, "tensor", sibling) for piece in own]
    peer = peer + [lax.ppermute(piece, "tensor", sibling) for piece in peer]
    weight = columns(out_proj.reshape(tensor_size, width, HD), inner, 1)

    work = 2 * 2 * rows * groups * rows * HD
    packed_shape = (HD + 16, 2 * rows)
    (packed,) = call(
        functools.partial(forward_kernel, groups),
        [(packed_shape, BF16)],
        [pltpu.VMEM((groups, rows, 2 * rows), F32)],
        2 * work,
        4 * rows * groups * HD,
    )(query_states, q_peer, *kvs)
    packed_theirs = lax.ppermute(packed, "context", pair)

    grad_mine, grad_sent = call(
        functools.partial(grad_kernel, tensor_size),
        [((2 * rows, HD), F32), ((2 * rows, HD), BF16)],
        [],
        2 * 2 * rows * width * tensor_size // 2 * HD,
        2 * rows * width * tensor_size,
    )(*own, *peer, weight)
    grad_theirs = lax.ppermute(grad_sent, "context", pair)

    attended, log_total, *parts = call(
        functools.partial(proj_kernel, tensor_size, groups, span),
        [((HD, 2 * rows), BF16), ((8, 2 * rows), F32), ((HD, span), F32)] + [((HD, span), BF16)] * (groups - 1),
        [pltpu.VMEM((groups, HD, span), F32)],
        2 * 2 * rows * width * tensor_size // 2 * HD,
        2 * rows * width * tensor_size,
    )(*own, *peer, packed, packed_theirs)
    parts = parts[:1] + [shifted(parts[n], n) for n in range(1, groups)]

    q_mine, q_sent, *pieces = call(
        functools.partial(backward_kernel, groups),
        [((HD, rows), F32), ((HD, rows), BF16), ((rows, 2 * HD), F32)] + [((rows, 2 * HD), BF16)] * (groups - 1),
        [],
        5 * work,
        8 * rows * groups * HD,
    )(query_states, q_peer, *kvs, grad_mine, grad_theirs, attended, log_total)
    q_theirs = lax.ppermute(q_sent, "context", pair)
    pieces = pieces[:1] + [shifted(pieces[n], -n) for n in range(1, groups)]

    query_grad, key_grad, value_grad = call(
        functools.partial(join_kernel, groups),
        [((rows, HD), BF16)] * 3,
        [],
        rows * HD * groups,
        4 * rows * HD * groups,
    )(q_mine, q_theirs, *pieces)
    (proj_grad,) = call(
        functools.partial(proj_join_kernel, groups),
        [((span, HD), F32)],
        [],
        span * HD * groups,
        2 * span * HD * groups,
    )(*parts)
    return (query_grad, key_grad, value_grad, proj_grad)


def solution(mesh):
    spec = P("context", "tensor")
    return jax.shard_map(
        functools.partial(local, mesh.shape["tensor"], mesh.shape["context"]),
        mesh=mesh,
        in_specs=(spec, spec, spec, spec, P(None, "tensor")),
        out_specs=(spec, spec, spec, spec),
        check_vma=False,
    )
```
